32 devices in a mesh: sub: 4 (over z), wide: 8 (over y, x, core).
Axes of the slice: x: 2, y: 2, z: 4, core: 2. Of those that a mesh axis runs over, the one named last changes fastest.
Arguments:
- load_table: bfloat16 [4, 8, 16, 4, 128], P('sub', 'wide'), may hold values from -6 to 6
- load_column: int32 [64], replicated, may hold values from 0 to 15
- face_order: int32 [4, 8, 4], P('sub', 'wide'), may hold values from 0 to 3, each once within a row
- schur: bfloat16 [4, 8, 512, 512], P('sub', 'wide'), as said below
- neumann: bfloat16 [4, 8, 512, 512], P('sub', 'wide'), as said below
- coarse_basis: bfloat16 [4, 8, 4, 4, 128], P('sub', 'wide'), may hold values from -0.625 to 0.625
- corner_map: int32 [4, 8, 4], P('sub', 'wide'), may hold values from 0 to 47, as said below
- coarse_inverse: float32 [48, 48], P('wide'), as said below
Outputs:
- solution: float32 [4, 8, 4, 64, 128], P('sub', 'wide')
The draws below stay inside these ranges and needn't reach their ends.
Inputs may be any that keep to these rules, and one draw needn't show every extreme that they name: `corner_map`: each subdomain's 4 entries are distinct; subdomains that meet at a corner of the grid of subdomains give it the same number, and different corners get different numbers, so (5) * (9) of the 48 numbers occur and the others belong to no corner. `coarse_inverse`: Symmetric. `schur`: Symmetric. `neumann`: Symmetric.
All inputs are finite; a program needn't handle non-finite values.
Results may differ from the reference program's by a relative error of at most 0.0014.
Values sent between devices are 32-bit elements; how exact they have to be, the bound alone decides.
A program may use at most 64 MiB of HBM per device.

```python
import math
import jax
import jax.numpy as jnp
from jax import lax

NI = 512
RHS = 64
NLOAD = 16
PRIM = 4
ITERS = 3
FB = 128
ROWS = 4
COLS = 8
NCOARSE = 48


def spd_blocks(key, lowest, highest, spread):
    key_diag, key_noise = jax.random.split(key)
    diagonal = jax.random.uniform(key_diag, (ROWS, COLS, NI), jnp.float32, lowest, highest)
    noise_part = jax.random.normal(key_noise, (ROWS, COLS, NI, NI), jnp.float32) * (spread / math.sqrt(2.0 * NI))
    symmetric = noise_part + jnp.swapaxes(noise_part, 2, 3)
    identity = jnp.eye(NI, dtype=jnp.float32)
    return (symmetric + diagonal[..., None] * identity).astype(jnp.bfloat16)


def draw_schur(key, part):
    return spd_blocks(jax.random.fold_in(key, 11), 1.0, 2.0, 0.35)


def draw_neumann(key, part):
    return spd_blocks(jax.random.fold_in(key, 23), 0.6, 1.2, 0.25)


def draw_coarse_inverse(key, part):
    key_diag, key_noise = jax.random.split(jax.random.fold_in(key, 37))
    lowest, highest, spread = (0.6, 1.2, 0.2)
    diagonal = jax.random.uniform(key_diag, (NCOARSE,), jnp.float32, lowest, highest)
    noise_part = jax.random.normal(key_noise, (NCOARSE, NCOARSE), jnp.float32) * (spread / math.sqrt(1.0 * NCOARSE))
    symmetric = noise_part + noise_part.T
    return symmetric + jnp.diag(diagonal)


def draw_corner_map(key, part):
    numbering = jax.random.permutation(jax.random.fold_in(key, 53), NCOARSE)
    corner_base = jnp.arange(ROWS)[:, None] * (COLS + 1) + jnp.arange(COLS)[None, :]
    corner_index = jnp.stack([corner_base, corner_base + 1, corner_base + COLS + 1, corner_base + COLS + 2], axis=-1)
    return numbering[corner_index].astype(jnp.int32)


def place_ends(array, stream_key, low, top_value):
    longest = array.shape.index(max(array.shape))
    spots = []
    for shift in (0, 1):
        where = [jax.random.randint(jax.random.fold_in(stream_key, axis), (), 0, length) for axis, length in enumerate(array.shape)]
        where[longest] = (where[longest] + shift) % array.shape[longest]
        spots.append(tuple(where))
    return array.at[spots[0]].set(low).at[spots[1]].set(top_value)


def level_of(stream_key, shape, cuts, smallest, largest):
    def one(position, shards_of):
        draws = jax.random.uniform(jax.random.fold_in(jax.random.fold_in(stream_key, 6), position), (shards_of,), jnp.float32, smallest / len(cuts), largest / len(cuts))
        return jnp.repeat(jnp.exp(draws), shape[position] // shards_of).reshape((-1,) + (1,) * (len(shape) - position - 1))

    gain = one(*cuts[0])
    for cut in cuts[1:]:
        gain = gain * one(*cut)
    return gain


def noise(stream_key, shape, scale, bound, cuts=(), kind=jnp.bfloat16):
    drawn = scale * jax.random.normal(stream_key, shape, jnp.float32)
    if cuts:
        drawn = drawn * level_of(stream_key, shape, cuts, -0.22, 0.18)
    return jnp.clip(drawn, -bound, bound).astype(kind)


def setup_inputs(seed: int = 0) -> dict:
    key_list = jax.random.split(jax.random.key(seed), 9)
    load_table = noise(key_list[0], (ROWS, COLS, NLOAD, 4, FB), 1.0, 6.0, ((0, 4), (1, 8)))
    load_column = place_ends(jax.random.randint(key_list[1], (RHS,), 0, NLOAD), jax.random.fold_in(key_list[1], 1), 0, NLOAD - 1).astype(jnp.int32)
    face_order = jax.vmap(lambda own: jax.random.permutation(own, 4))(jax.random.split(key_list[2], ROWS * COLS)).reshape((ROWS, COLS, 4)).astype(jnp.int32)
    schur = draw_schur(jax.random.fold_in(key_list[8], 71), 0)
    neumann = draw_neumann(jax.random.fold_in(key_list[8], 71), 0)
    coarse_basis = noise(key_list[5], (ROWS, COLS, PRIM, 4, FB), (NI // 5) ** -0.5, 0.625, ((0, 4), (1, 8)))
    corner_map = draw_corner_map(jax.random.fold_in(key_list[8], 71), 0)
    coarse_inverse = draw_coarse_inverse(jax.random.fold_in(key_list[8], 71), 0)
    return dict(load_table=load_table, load_column=load_column, face_order=face_order, schur=schur, neumann=neumann, coarse_basis=coarse_basis, corner_map=corner_map, coarse_inverse=coarse_inverse)


damping = 0.3


def share_weights():
    row_index = jnp.arange(ROWS)[:, None] * jnp.ones((1, COLS), jnp.int32)
    col_index = jnp.ones((ROWS, 1), jnp.int32) * jnp.arange(COLS)[None, :]
    half = jnp.float32(0.5)
    whole = jnp.float32(1.0)
    north_share = jnp.where(row_index > 0, half, whole)
    south_share = jnp.where(row_index < ROWS - 1, half, whole)
    west_share = jnp.where(col_index > 0, half, whole)
    east_share = jnp.where(col_index < COLS - 1, half, whole)
    return jnp.stack([north_share, south_share, west_share, east_share], axis=2)[:, :, :, None, None]


def assemble(copies):
    empty_row = jnp.zeros_like(copies[:1, :, 0])
    empty_col = jnp.zeros_like(copies[:, :1, 0])
    upper_faces = jnp.concatenate([empty_row, copies[:-1, :, 1]], axis=0)
    lower_faces = jnp.concatenate([copies[1:, :, 0], empty_row], axis=0)
    left_faces = jnp.concatenate([empty_col, copies[:, :-1, 3]], axis=1)
    right_faces = jnp.concatenate([copies[:, 1:, 2], empty_col], axis=1)
    return jnp.stack([copies[:, :, 0] + upper_faces, copies[:, :, 1] + lower_faces,
                      copies[:, :, 2] + left_faces, copies[:, :, 3] + right_faces], axis=2)


def apply_local(vectors, operators, face_order):
    selector = (face_order[..., :, None] == jnp.arange(4, dtype=jnp.int32)).astype(jnp.float32)
    rounded = lax.optimization_barrier(vectors.astype(jnp.bfloat16)).astype(jnp.float32)
    blocked = jnp.einsum('rcbf,rcfjn->rcjbn', selector, rounded, precision=lax.Precision.HIGHEST)
    blocked = blocked.reshape(ROWS * COLS, RHS, NI).astype(jnp.bfloat16)
    flat_ops = operators.reshape(ROWS * COLS, NI, NI)
    product = lax.map(lambda operands: jnp.dot(operands[0], operands[1], preferred_element_type=jnp.float32),
                      (blocked, flat_ops))
    product = product.reshape(ROWS, COLS, RHS, 4, FB)
    return jnp.einsum('rcbf,rcjbn->rcfjn', selector, product, precision=lax.Precision.HIGHEST)


def reference(load_table, load_column, face_order, schur, neumann, coarse_basis, corner_map, coarse_inverse):
    load_select = (load_column[:, None] == jnp.arange(NLOAD, dtype=jnp.int32)).astype(jnp.float32)
    load_faces = jnp.einsum('jl,rclfn->rcfjn', load_select, load_table.astype(jnp.float32),
                            precision=lax.Precision.HIGHEST)
    weights = share_weights()
    basis = coarse_basis.astype(jnp.float32)
    solution = jnp.zeros((ROWS, COLS, 4, RHS, FB), jnp.float32)
    for iteration in range(ITERS):
        if iteration == 0:
            residual = assemble(load_faces)
        else:
            residual = assemble(load_faces - apply_local(solution, schur, face_order))
        weighted = weights * residual
        restricted = jnp.einsum('rcpfn,rcfjn->rcpj', basis, weighted, precision=lax.Precision.HIGHEST)
        coarse_residual = jax.ops.segment_sum(restricted.reshape(ROWS * COLS * PRIM, RHS),
                                              corner_map.reshape(ROWS * COLS * PRIM), NCOARSE)
        coarse_solution = jnp.dot(coarse_residual.T, coarse_inverse, precision=lax.Precision.HIGHEST)
        picked = coarse_solution[:, corner_map]
        correction = jnp.einsum('jrcp,rcpfn->rcfjn', picked, basis, precision=lax.Precision.HIGHEST)
        neumann_part = apply_local(weighted, neumann, face_order)
        update = assemble(weights * (neumann_part + correction))
        solution = solution + damping * update
    return solution
```

```python
import functools

import jax
import jax.numpy as jnp
from jax import lax
from jax.experimental import pallas as pl
from jax.experimental.pallas import tpu as pltpu
from jax.sharding import PartitionSpec as P

ITERS = 3
damping = 0.3
MESH = pl.DeviceIdType.MESH
HIGHEST = lax.Precision.HIGHEST
OPPOSITE = (1, 0, 3, 2)


def split(value):
    high = value.astype(jnp.bfloat16)
    low = (value - high.astype(jnp.float32)).astype(jnp.bfloat16)
    return high, low


def dot(a, b, dims, precision=None):
    return lax.dot_general(
        a, b, (dims, ((), ())), precision=precision, preferred_element_type=jnp.float32
    )


def kernel(
    sizes,
    face_order,
    corner_map,
    load_column,
    load_table,
    basis_in,
    inverse_in,
    schur_hbm,
    neumann_hbm,
    out,
    schur,
    neumann,
    load,
    sol,
    face_out,
    face_in,
    basis_out,
    basis_near,
    corner_all,
    corner_flat,
    inverse_all,
    inverse_flat,
    gmat,
    hmat,
    rest_all,
    rest_flat,
    local_sem,
    face_send,
    face_recv,
    basis_send,
    basis_recv,
    corner_send,
    corner_recv,
    inverse_send,
    inverse_recv,
    rest_send,
    rest_recv,
):
    subs, wides = sizes
    devices = subs * wides
    rhs, width = sol.shape[1], sol.shape[2]
    prims = basis_out.shape[1]
    order = inverse_flat.shape[0]
    owned = inverse_in.shape[0]
    row = lax.axis_index("sub")
    col = lax.axis_index("wide")
    me = row * wides + col
    has = (row > 0, row < subs - 1, col > 0, col < wides - 1)
    near = ((row - 1, col), (row + 1, col), (row, col - 1), (row, col + 1))
    share = [jnp.where(flag, jnp.float32(0.5), jnp.float32(1.0)) for flag in has]

    def place(step):
        peer = lax.rem(me + step, devices)
        return peer, (peer // wides, lax.rem(peer, wides))

    def each_peer(action):
        def one(step, carry):
            action(*place(step))
            return carry

        lax.fori_loop(1, devices, one, 0)

    load_n = pltpu.make_async_copy(neumann_hbm, neumann, local_sem.at[0])
    load_s = pltpu.make_async_copy(schur_hbm, schur, local_sem.at[1])
    load_n.start()
    load_s.start()

    barrier = pltpu.get_barrier_semaphore()
    each_peer(
        lambda peer, where: pl.semaphore_signal(
            barrier, inc=1, device_id=where, device_id_type=MESH
        )
    )

    basis = basis_in[...].astype(jnp.float32)
    for f in range(4):
        basis_out[f] = jnp.concatenate(
            [basis[4 * p + f : 4 * p + f + 1] for p in range(prims)], axis=0
        )
    row_of = lax.broadcasted_iota(jnp.int32, (prims, 128), 0)
    marks = jnp.zeros((prims, 128), jnp.int32)
    for p in range(prims):
        marks = jnp.where(row_of == p, corner_map[p], marks)
    corner_all[me] = marks
    table = load_table[...]
    wanted = load_column[...] * 4
    pattern = lax.broadcasted_iota(jnp.int32, (table.shape[0], rhs), 0)
    for f in range(4):
        chosen = (pattern == wanted + f).astype(jnp.float32)
        load[f] = dot(chosen.T.astype(jnp.bfloat16), table, ((1,), (0,)))
        face_out[0, f] = load[f]
    inverse_all[col] = inverse_in[...]
    for f in range(4):

        @pl.when(jnp.logical_not(has[f]))
        def _():
            for turn in range(2 * ITERS):
                face_in[turn, f] = jnp.zeros((rhs, width), jnp.float32)
            basis_near[f] = jnp.zeros((prims, width), jnp.float32)

    pl.semaphore_wait(barrier, devices - 1)

    def face_copy(turn, f):
        return pltpu.make_async_remote_copy(
            src_ref=face_out.at[turn, f],
            dst_ref=face_in.at[turn, OPPOSITE[f]],
            send_sem=face_send.at[turn, f],
            recv_sem=face_recv.at[turn, OPPOSITE[f]],
            device_id=near[f],
            device_id_type=MESH,
        )

    def face_wait(turn, f):
        pltpu.make_async_copy(
            face_out.at[turn, f], face_in.at[turn, f], face_recv.at[turn, f]
        ).wait()

    def basis_copy(f):
        return pltpu.make_async_remote_copy(
            src_ref=basis_out.at[f],
            dst_ref=basis_near.at[OPPOSITE[f]],
            send_sem=basis_send.at[f],
            recv_sem=basis_recv.at[OPPOSITE[f]],
            device_id=near[f],
            device_id_type=MESH,
        )

    def corner_copy(peer, where):
        return pltpu.make_async_remote_copy(
            src_ref=corner_all.at[me],
            dst_ref=corner_all.at[me],
            send_sem=corner_send.at[0],
            recv_sem=corner_recv.at[0],
            device_id=where,
            device_id_type=MESH,
        )

    def inverse_copy(other):
        return pltpu.make_async_remote_copy(
            src_ref=inverse_all.at[col],
            dst_ref=inverse_all.at[col],
            send_sem=inverse_send.at[other],
            recv_sem=inverse_recv.at[col],
            device_id=(row, other),
            device_id_type=MESH,
        )

    def rest_copy(iteration, peer, where):
        return pltpu.make_async_remote_copy(
            src_ref=rest_all.at[iteration, me],
            dst_ref=rest_all.at[iteration, me],
            send_sem=rest_send.at[iteration],
            recv_sem=rest_recv.at[iteration],
            device_id=where,
            device_id_type=MESH,
        )

    def wait_others(blocks, sem):
        others = blocks.at[pl.ds(0, devices - 1)]
        pltpu.make_async_copy(others, others, sem).wait()

    def send_faces(turn):
        for f in (0, 1, 2, 3):

            @pl.when(has[f])
            def _():
                face_copy(turn, f).start()

    def wait_faces(turn):
        for f in (0, 1, 2, 3):

            @pl.when(has[f])
            def _():
                face_wait(turn, f)

    send_faces(0)
    for f in range(4):

        @pl.when(has[f])
        def _():
            basis_copy(f).start()

    each_peer(lambda peer, where: corner_copy(peer, where).start())

    def each_wide(action):
        def one(step, carry):
            action(lax.rem(col + step, wides))
            return carry

        lax.fori_loop(1, wides, one, 0)

    each_wide(lambda other: inverse_copy(other).start())

    order_of = [jnp.full((rhs, width), face_order[b], jnp.int32) for b in range(4)]
    held = [[order_of[b] == f for f in range(4)] for b in range(4)]

    def pick(masks, values):
        chosen = values[3]
        for i in range(3):
            chosen = jnp.where(masks[i], values[i], chosen)
        return chosen

    def apply_local(vectors, operator):
        blocked = jnp.concatenate(
            [pick(held[b], vectors).astype(jnp.bfloat16) for b in range(4)], axis=1
        )
        result = dot(blocked, operator[...], ((1,), (0,)))
        parts = [result[:, b * width : (b + 1) * width] for b in range(4)]
        return [pick([held[b][f] for b in range(4)], parts) for f in range(4)]

    own_basis = jnp.concatenate([basis_out[f] for f in range(4)], axis=1)
    own_half = own_basis.astype(jnp.bfloat16)
    group = min(devices, 32)
    span = group * prims

    def prepare():
        each_wide(
            lambda other: pltpu.make_async_copy(
                inverse_all.at[other], inverse_all.at[other], inverse_recv.at[other]
            ).wait()
        )
        for w in range(wides):
            inverse_flat[w * owned : (w + 1) * owned, :] = inverse_all[w]
        for f in range(4):

            @pl.when(has[f])
            def _():
                pltpu.make_async_copy(
                    basis_near.at[f], basis_near.at[f], basis_recv.at[f]
                ).wait()

        wait_others(corner_all, corner_recv.at[0])
        gmat[...] = jnp.zeros(gmat.shape, jnp.float32)
        gmat[0:prims, :] = own_basis
        for f in range(4):
            gmat[(f + 1) * prims : (f + 2) * prims, f * width : (f + 1) * width] = basis_near[f]
        lanes = lax.broadcasted_iota(jnp.int32, (prims, order), 1)
        picks = [marks[:, :1] == lanes]
        for f in range(4):
            peer = jnp.where(has[f], near[f][0] * wides + near[f][1], me)
            picks.append(corner_all[peer][:, :1] == lanes)
        mine = jnp.concatenate([pick.astype(jnp.float32) for pick in picks], axis=0)
        columns = dot(mine, inverse_flat[...], ((1,), (0,)), HIGHEST)
        spread = dot(columns.T, gmat[0 : 5 * prims, :], ((1,), (0,)), HIGHEST)

        def one(part):
            for d in range(group):
                corner_flat[d * prims : (d + 1) * prims, :] = corner_all[part * group + d]
            wide_lanes = lax.broadcasted_iota(jnp.int32, (span, order), 1)
            chosen = (corner_flat[:, :1] == wide_lanes).astype(jnp.float32)
            hmat[pl.ds(pl.multiple_of(part * span, span), span), :] = dot(
                chosen, spread, ((1,), (0,)), HIGHEST
            )

        if devices == group:
            one(0)
        else:
            lax.fori_loop(0, devices // group, lambda part, carry: (one(part), carry)[1], 0)

    def correct(iteration):
        def one(part):
            for d in range(group):
                rest_flat[d * prims : (d + 1) * prims, :] = rest_all[iteration, part * group + d]
            return dot(
                rest_flat[...].T,
                hmat[pl.ds(pl.multiple_of(part * span, span), span), :],
                ((1,), (0,)),
                HIGHEST,
            )

        if devices == group:
            return one(0)
        return lax.fori_loop(
            0,
            devices // group,
            lambda part, total: total + one(part),
            jnp.zeros((rhs, 4 * width), jnp.float32),
        )

    for iteration in range(ITERS):
        first = 2 * iteration
        if iteration > 0:
            if iteration == 1:
                load_s.wait()
            local = apply_local([sol[f] for f in range(4)], schur)
            for f in range(4):
                face_out[first, f] = load[f] - local[f]
            send_faces(first)
        wait_faces(first)
        weighted = [share[f] * (face_out[first, f] + face_in[first, f]) for f in range(4)]
        high, low = split(jnp.concatenate(weighted, axis=1))
        restricted = dot(own_half, high, ((1,), (1,))) + dot(own_half, low, ((1,), (1,)))
        rest_all[iteration, me] = restricted
        each_peer(lambda peer, where: rest_copy(iteration, peer, where).start())
        if iteration == 0:
            load_n.wait()
        local = apply_local(weighted, neumann)
        for f in range(4):
            face_out[first + 1, f] = local[f]
        send_faces(first + 1)
        if iteration == 0:
            prepare()
        wait_others(rest_all.at[iteration], rest_recv.at[iteration])
        correction = correct(iteration)
        wait_faces(first + 1)
        for f in range(4):
            update = share[f] * (
                face_out[first + 1, f]
                + face_in[first + 1, f]
                + correction[:, f * width : (f + 1) * width]
            )
            if iteration == 0:
                sol[f] = damping * update
            elif iteration < ITERS - 1:
                sol[f] = sol[f] + damping * update
            else:
                out[f] = sol[f] + damping * update

    for turn in range(2 * ITERS):
        for f in range(4):

            @pl.when(has[f])
            def _():
                face_copy(turn, f).wait_send()

    for f in range(4):

        @pl.when(has[f])
        def _():
            basis_copy(f).wait_send()

    each_wide(lambda other: inverse_copy(other).wait_send())

    wait_others(corner_all, corner_send.at[0])
    for iteration in range(ITERS):
        wait_others(rest_all.at[iteration], rest_send.at[iteration])


def body(
    load_table, load_column, face_order, schur, neumann, coarse_basis, corner_map, coarse_inverse
):
    subs, wides = lax.axis_size("sub"), lax.axis_size("wide")
    devices = subs * wides
    patterns, width = load_table.shape[2], load_table.shape[4]
    rhs = load_column.shape[0]
    inner = schur.shape[2]
    prims = coarse_basis.shape[2]
    owned, order = coarse_inverse.shape
    assert schur.shape[0] == 1 and schur.shape[1] == 1
    f32 = jnp.float32
    group = min(devices, 32)
    dma = pltpu.SemaphoreType.DMA
    vmem = pl.BlockSpec(memory_space=pltpu.VMEM)
    smem = pl.BlockSpec(memory_space=pltpu.SMEM)
    hbm = pl.BlockSpec(memory_space=pl.ANY)
    result = pl.pallas_call(
        functools.partial(kernel, (subs, wides)),
        out_shape=jax.ShapeDtypeStruct((4, rhs, width), f32),
        in_specs=[smem, smem, vmem, vmem, vmem, vmem, hbm, hbm],
        out_specs=vmem,
        scratch_shapes=[
            pltpu.VMEM((inner, inner), schur.dtype),
            pltpu.VMEM((inner, inner), neumann.dtype),
            pltpu.VMEM((4, rhs, width), f32),
            pltpu.VMEM((4, rhs, width), f32),
            pltpu.VMEM((2 * ITERS, 4, rhs, width), f32),
            pltpu.VMEM((2 * ITERS, 4, rhs, width), f32),
            pltpu.VMEM((4, prims, width), f32),
            pltpu.VMEM((4, prims, width), f32),
            pltpu.VMEM((devices, prims, 128), jnp.int32),
            pltpu.VMEM((group * prims, 128), jnp.int32),
            pltpu.VMEM((wides, owned, order), f32),
            pltpu.VMEM((order, order), f32),
            pltpu.VMEM((5 * prims, 4 * width), f32),
            pltpu.VMEM((devices * prims, 4 * width), f32),
            pltpu.VMEM((ITERS, devices, prims, rhs), f32),
            pltpu.VMEM((group * prims, rhs), f32),
            dma((2,)),
            dma((2 * ITERS, 4)),
            dma((2 * ITERS, 4)),
            dma((4,)),
            dma((4,)),
            dma((1,)),
            dma((1,)),
            dma((wides,)),
            dma((wides,)),
            dma((ITERS,)),
            dma((ITERS,)),
        ],
        compiler_params=pltpu.CompilerParams(collective_id=0, has_side_effects=True),
        name="bddc",
    )(
        face_order.reshape(4),
        corner_map.reshape(prims),
        load_column.reshape(1, rhs),
        load_table.reshape(patterns * 4, width),
        coarse_basis.reshape(prims * 4, width),
        coarse_inverse,
        schur.reshape(inner, inner),
        neumann.reshape(inner, inner),
    )
    return result.reshape(1, 1, 4, rhs, width)


def solution(mesh):
    in_specs = (
        P("sub", "wide", None, None, None),
        P(),
        P("sub", "wide", None),
        P("sub", "wide", None, None),
        P("sub", "wide", None, None),
        P("sub", "wide", None, None, None),
        P("sub", "wide", None),
        P("wide", None),
    )
    out_specs = P("sub", "wide", None, None, None)
    return jax.shard_map(body, mesh=mesh, in_specs=in_specs, out_specs=out_specs, check_vma=False)
```

```python
import functools

import jax
import jax.numpy as jnp
from jax import lax
from jax.experimental import pallas as pl
from jax.experimental.pallas import tpu as pltpu
from jax.sharding import PartitionSpec as P

ITERS = 3
damping = 0.3
MESH = pl.DeviceIdType.MESH
HIGHEST = lax.Precision.HIGHEST
OPPOSITE = (1, 0, 3, 2)


def split(value):
    high = value.astype(jnp.bfloat16)
    low = (value - high.astype(jnp.float32)).astype(jnp.bfloat16)
    return high, low


def dot(a, b, dims, precision=None):
    return lax.dot_general(
        a, b, (dims, ((), ())), precision=precision, preferred_element_type=jnp.float32
    )


def kernel(
    sizes,
    face_order,
    corner_map,
    load_table,
    basis_in,
    inverse_in,
    schur_hbm,
    neumann_hbm,
    out,
    schur,
    neumann,
    load,
    sol,
    face_out,
    face_in,
    basis_out,
    basis_near,
    corner_all,
    corner_flat,
    inverse_all,
    inverse_flat,
    gmat,
    spread,
    hot,
    rest_all,
    rest_flat,
    far_sem,
    local_sem,
    face_send,
    face_recv,
    basis_send,
    basis_recv,
    corner_send,
    corner_recv,
    inverse_send,
    inverse_recv,
    rest_send,
    rest_recv,
):
    subs, wides = sizes
    devices = subs * wides
    rhs, width = sol.shape[1], sol.shape[2]
    prims = basis_out.shape[1]
    order = inverse_flat.shape[0]
    owned = inverse_in.shape[0]
    row = lax.axis_index("sub")
    col = lax.axis_index("wide")
    me = row * wides + col
    has = (row > 0, row < subs - 1, col > 0, col < wides - 1)
    near = ((row - 1, col), (row + 1, col), (row, col - 1), (row, col + 1))
    share = [jnp.where(flag, jnp.float32(0.5), jnp.float32(1.0)) for flag in has]

    def place(step):
        peer = lax.rem(me + step, devices)
        return peer, (peer // wides, lax.rem(peer, wides))

    def each_peer(action):
        def one(step, carry):
            action(*place(step))
            return carry

        lax.fori_loop(1, devices, one, 0)

    load_n = pltpu.make_async_copy(neumann_hbm, neumann, local_sem.at[0])
    load_s = pltpu.make_async_copy(schur_hbm, schur, local_sem.at[1])
    load_n.start()
    load_s.start()

    def loop(count, action):
        def one(step, carry):
            action(step)
            return carry

        lax.fori_loop(1, count, one, 0)

    def each_wide(action):
        loop(wides, lambda step: action(lax.rem(col + step, wides)))

    def each_sub(action):
        loop(subs, lambda step: action(lax.rem(row + step, subs)))

    barrier = pltpu.get_barrier_semaphore()

    def signal(sem, where):
        pl.semaphore_signal(sem, inc=1, device_id=where, device_id_type=MESH)

    each_sub(lambda other: signal(barrier, (other, col)))
    each_wide(lambda other: signal(barrier, (row, other)))

    basis = basis_in[...].astype(jnp.float32)
    for f in range(4):
        basis_out[f] = jnp.concatenate(
            [basis[4 * p + f : 4 * p + f + 1] for p in range(prims)], axis=0
        )
    row_of = lax.broadcasted_iota(jnp.int32, (prims, 128), 0)
    marks = jnp.zeros((prims, 128), jnp.int32)
    for p in range(prims):
        marks = jnp.where(row_of == p, corner_map[p], marks)
    corner_all[me] = marks
    table = load_table[...]
    target = 4 * lax.broadcasted_iota(jnp.int32, (rhs, table.shape[0]), 0)
    source = lax.broadcasted_iota(jnp.int32, (rhs, table.shape[0]), 1)
    for f in range(4):
        chosen = (source == target + f).astype(jnp.bfloat16)
        load[f] = dot(chosen, table, ((1,), (0,)))
        face_out[0, f] = load[f]
    inverse_all[col] = inverse_in[...]
    for f in range(4):

        @pl.when(jnp.logical_not(has[f]))
        def _():
            for turn in range(2 * ITERS):
                face_in[turn, f] = jnp.zeros((rhs, width), jnp.float32)
            basis_near[f] = jnp.zeros((prims, width), jnp.float32)

    pl.semaphore_wait(barrier, subs - 1 + wides - 1)
    each_sub(lambda other: signal(far_sem, (other, col)))

    def face_copy(turn, f):
        return pltpu.make_async_remote_copy(
            src_ref=face_out.at[turn, f],
            dst_ref=face_in.at[turn, OPPOSITE[f]],
            send_sem=face_send.at[turn, f],
            recv_sem=face_recv.at[turn, OPPOSITE[f]],
            device_id=near[f],
            device_id_type=MESH,
        )

    def face_wait(turn, f):
        pltpu.make_async_copy(
            face_out.at[turn, f], face_in.at[turn, f], face_recv.at[turn, f]
        ).wait()

    def basis_copy(f):
        return pltpu.make_async_remote_copy(
            src_ref=basis_out.at[f],
            dst_ref=basis_near.at[OPPOSITE[f]],
            send_sem=basis_send.at[f],
            recv_sem=basis_recv.at[OPPOSITE[f]],
            device_id=near[f],
            device_id_type=MESH,
        )

    def corner_copy(peer, where):
        return pltpu.make_async_remote_copy(
            src_ref=corner_all.at[me],
            dst_ref=corner_all.at[me],
            send_sem=corner_send.at[0],
            recv_sem=corner_recv.at[0],
            device_id=where,
            device_id_type=MESH,
        )

    def inverse_copy(other):
        return pltpu.make_async_remote_copy(
            src_ref=inverse_all.at[col],
            dst_ref=inverse_all.at[col],
            send_sem=inverse_send.at[other],
            recv_sem=inverse_recv.at[col],
            device_id=(row, other),
            device_id_type=MESH,
        )

    def rest_copy(iteration, peer, where):
        return pltpu.make_async_remote_copy(
            src_ref=rest_all.at[iteration, me],
            dst_ref=rest_all.at[iteration, me],
            send_sem=rest_send.at[iteration],
            recv_sem=rest_recv.at[iteration],
            device_id=where,
            device_id_type=MESH,
        )

    def wait_others(blocks, sem):
        others = blocks.at[pl.ds(0, devices - 1)]
        pltpu.make_async_copy(others, others, sem).wait()

    def send_faces(turn):
        for f in (0, 1, 2, 3):

            @pl.when(has[f])
            def _():
                face_copy(turn, f).start()

    def wait_faces(turn):
        for f in (0, 1, 2, 3):

            @pl.when(has[f])
            def _():
                face_wait(turn, f)

    for f in range(4):

        @pl.when(has[f])
        def _():
            basis_copy(f).start()

    send_faces(0)
    each_wide(lambda other: inverse_copy(other).start())
    pl.semaphore_wait(far_sem, subs - 1)
    each_peer(lambda peer, where: corner_copy(peer, where).start())

    order_of = [jnp.full((rhs, width), face_order[b], jnp.int32) for b in range(4)]
    held = [[order_of[b] == f for f in range(4)] for b in range(4)]

    def pick(masks, values):
        chosen = values[3]
        for i in range(3):
            chosen = jnp.where(masks[i], values[i], chosen)
        return chosen

    def apply_local(vectors, operator):
        blocked = jnp.concatenate(
            [pick(held[b], vectors).astype(jnp.bfloat16) for b in range(4)], axis=1
        )
        result = dot(blocked, operator[...], ((1,), (0,)))
        parts = [result[:, b * width : (b + 1) * width] for b in range(4)]
        return [pick([held[b][f] for b in range(4)], parts) for f in range(4)]

    own_basis = jnp.concatenate([basis_out[f] for f in range(4)], axis=1)
    gmat[...] = jnp.zeros(gmat.shape, jnp.float32)
    gmat[0:prims, :] = own_basis
    for f in range(4):

        @pl.when(has[f])
        def _():
            pltpu.make_async_copy(basis_near.at[f], basis_near.at[f], basis_recv.at[f]).wait()

    for f in range(4):
        gmat[(f + 1) * prims : (f + 2) * prims, f * width : (f + 1) * width] = basis_near[f]
    sides = jnp.ones((1, width), jnp.float32)
    weights = jnp.concatenate([share[f] * sides for f in range(4)], axis=1)
    shared = (gmat[...] * weights).astype(jnp.bfloat16)
    group = min(devices, 32)
    span = group * prims
    shifts = (0, -wides, wides, -1, 1)

    def restrict(values):
        high, low = split(values)
        parts = dot(shared, high, ((1,), (1,))) + dot(shared, low, ((1,), (1,)))
        return jnp.concatenate([parts[g * prims : (g + 1) * prims] for g in range(5)], axis=1)

    def mark(part):
        for g in range(5):
            for d in range(group):
                peer = jnp.clip(part * group + d + shifts[g], 0, devices - 1)
                start = g * span + d * prims
                corner_flat[start : start + prims, :] = corner_all[peer]
        lanes = lax.broadcasted_iota(jnp.int32, hot.shape, 1)
        hot[...] = (corner_flat[:, :1] == lanes).astype(jnp.float32).astype(jnp.bfloat16)

    def prepare():
        each_wide(
            lambda other: pltpu.make_async_copy(
                inverse_all.at[other], inverse_all.at[other], inverse_recv.at[other]
            ).wait()
        )
        for w in range(wides):
            inverse_flat[w * owned : (w + 1) * owned, :] = inverse_all[w]
        wait_others(corner_all, corner_recv.at[0])
        lanes = lax.broadcasted_iota(jnp.int32, (prims, order), 1)
        picks = [marks[:, :1] == lanes]
        for f in range(4):
            peer = jnp.where(has[f], near[f][0] * wides + near[f][1], me)
            picks.append(corner_all[peer][:, :1] == lanes)
        mine = jnp.concatenate([chosen.astype(jnp.float32) for chosen in picks], axis=0)
        columns = dot(mine, inverse_flat[...], ((1,), (0,)), HIGHEST)
        spread[...] = dot(columns.T, gmat[...], ((1,), (0,)), HIGHEST)
        if devices == group:
            mark(0)

    def correct(iteration):
        def one(part):
            if devices > group:
                mark(part)
            for d in range(group):
                rest_flat[d * prims : (d + 1) * prims, :] = rest_all[iteration, part * group + d]
            turned = rest_flat[...].T
            lined = jnp.concatenate([turned[g * rhs : (g + 1) * rhs] for g in range(5)], axis=1)
            high, low = split(lined)
            return dot(high, hot[...], ((1,), (0,))) + dot(low, hot[...], ((1,), (0,)))

        if devices == group:
            total = one(0)
        else:
            total = lax.fori_loop(
                0,
                devices // group,
                lambda part, total: total + one(part),
                jnp.zeros((rhs, order), jnp.float32),
            )
        return dot(total, spread[...], ((1,), (0,)), HIGHEST)

    for iteration in range(ITERS):
        first = 2 * iteration
        if iteration > 0:
            if iteration == 1:
                load_s.wait()
            local = apply_local([sol[f] for f in range(4)], schur)
            for f in range(4):
                face_out[first, f] = load[f] - local[f]
            send_faces(first)
        rest_all[iteration, me] = restrict(
            jnp.concatenate([face_out[first, f] for f in range(4)], axis=1)
        )
        each_peer(lambda peer, where: rest_copy(iteration, peer, where).start())
        wait_faces(first)
        weighted = [share[f] * (face_out[first, f] + face_in[first, f]) for f in range(4)]
        if iteration == 0:
            load_n.wait()
        local = apply_local(weighted, neumann)
        for f in range(4):
            face_out[first + 1, f] = local[f]
        send_faces(first + 1)
        if iteration == 0:
            prepare()
        wait_others(rest_all.at[iteration], rest_recv.at[iteration])
        correction = correct(iteration)
        wait_faces(first + 1)
        for f in range(4):
            update = share[f] * (
                face_out[first + 1, f]
                + face_in[first + 1, f]
                + correction[:, f * width : (f + 1) * width]
            )
            if iteration == 0:
                sol[f] = damping * update
            elif iteration < ITERS - 1:
                sol[f] = sol[f] + damping * update
            else:
                out[f] = sol[f] + damping * update

    for turn in range(2 * ITERS):
        for f in range(4):

            @pl.when(has[f])
            def _():
                face_copy(turn, f).wait_send()

    for f in range(4):

        @pl.when(has[f])
        def _():
            basis_copy(f).wait_send()

    each_wide(lambda other: inverse_copy(other).wait_send())

    wait_others(corner_all, corner_send.at[0])
    for iteration in range(ITERS):
        wait_others(rest_all.at[iteration], rest_send.at[iteration])


def expand(load_column, values, out):
    faces, patterns, width = values.shape
    rhs = out.shape[1]
    wanted = lax.broadcasted_iota(jnp.int32, (patterns, rhs), 0) == load_column[...]
    chosen = wanted.astype(jnp.float32).T.astype(jnp.bfloat16)
    whole = jnp.concatenate([values[f] for f in range(faces)], axis=1)
    high, low = split(whole)
    last = (whole - high.astype(jnp.float32) - low.astype(jnp.float32)).astype(jnp.bfloat16)
    result = (
        dot(chosen, high, ((1,), (0,)))
        + dot(chosen, low, ((1,), (0,)))
        + dot(chosen, last, ((1,), (0,)))
    )
    for f in range(faces):
        out[f] = result[:, f * width : (f + 1) * width]


def body(
    load_table, load_column, face_order, schur, neumann, coarse_basis, corner_map, coarse_inverse
):
    subs, wides = lax.axis_size("sub"), lax.axis_size("wide")
    devices = subs * wides
    patterns, width = load_table.shape[2], load_table.shape[4]
    rhs = load_column.shape[0]
    inner = schur.shape[2]
    prims = coarse_basis.shape[2]
    owned, order = coarse_inverse.shape
    assert schur.shape[0] == 1 and schur.shape[1] == 1
    f32 = jnp.float32
    group = min(devices, 32)
    dma = pltpu.SemaphoreType.DMA
    vmem = pl.BlockSpec(memory_space=pltpu.VMEM)
    smem = pl.BlockSpec(memory_space=pltpu.SMEM)
    hbm = pl.BlockSpec(memory_space=pl.ANY)
    result = pl.pallas_call(
        functools.partial(kernel, (subs, wides)),
        out_shape=jax.ShapeDtypeStruct((4, patterns, width), f32),
        in_specs=[smem, smem, vmem, vmem, vmem, hbm, hbm],
        out_specs=vmem,
        scratch_shapes=[
            pltpu.VMEM((inner, inner), schur.dtype),
            pltpu.VMEM((inner, inner), neumann.dtype),
            pltpu.VMEM((4, patterns, width), f32),
            pltpu.VMEM((4, patterns, width), f32),
            pltpu.VMEM((2 * ITERS, 4, patterns, width), f32),
            pltpu.VMEM((2 * ITERS, 4, patterns, width), f32),
            pltpu.VMEM((4, prims, width), f32),
            pltpu.VMEM((4, prims, width), f32),
            pltpu.VMEM((devices, prims, 128), jnp.int32),
            pltpu.VMEM((5 * group * prims, 128), jnp.int32),
            pltpu.VMEM((wides, owned, order), f32),
            pltpu.VMEM((order, order), f32),
            pltpu.VMEM((5 * prims, 4 * width), f32),
            pltpu.VMEM((order, 4 * width), f32),
            pltpu.VMEM((5 * group * prims, order), jnp.bfloat16),
            pltpu.VMEM((ITERS, devices, prims, 5 * patterns), f32),
            pltpu.VMEM((group * prims, 5 * patterns), f32),
            pltpu.SemaphoreType.REGULAR,
            dma((2,)),
            dma((2 * ITERS, 4)),
            dma((2 * ITERS, 4)),
            dma((4,)),
            dma((4,)),
            dma((1,)),
            dma((1,)),
            dma((wides,)),
            dma((wides,)),
            dma((ITERS,)),
            dma((ITERS,)),
        ],
        compiler_params=pltpu.CompilerParams(collective_id=0, has_side_effects=True),
        name="bddc",
    )(
        face_order.reshape(4),
        corner_map.reshape(prims),
        load_table.reshape(patterns * 4, width),
        coarse_basis.reshape(prims * 4, width),
        coarse_inverse,
        schur.reshape(inner, inner),
        neumann.reshape(inner, inner),
    )
    full = pl.pallas_call(
        expand,
        out_shape=jax.ShapeDtypeStruct((4, rhs, width), f32),
        in_specs=[vmem, vmem],
        out_specs=vmem,
        name="expand",
    )(load_column.reshape(1, rhs), result)
    return full.reshape(1, 1, 4, rhs, width)


def solution(mesh):
    in_specs = (
        P("sub", "wide", None, None, None),
        P(),
        P("sub", "wide", None),
        P("sub", "wide", None, None),
        P("sub", "wide", None, None),
        P("sub", "wide", None, None, None),
        P("sub", "wide", None),
        P("wide", None),
    )
    out_specs = P("sub", "wide", None, None, None)
    return jax.shard_map(body, mesh=mesh, in_specs=in_specs, out_specs=out_specs, check_vma=False)
```

```python
import functools

import jax
import jax.numpy as jnp
from jax import lax
from jax.experimental import pallas as pl
from jax.experimental.pallas import tpu as pltpu
from jax.sharding import PartitionSpec as P

ITERS = 3
damping = 0.3
MESH = pl.DeviceIdType.MESH
HIGHEST = lax.Precision.HIGHEST
OPPOSITE = (1, 0, 3, 2)


def split(value):
    high = value.astype(jnp.bfloat16)
    low = (value - high.astype(jnp.float32)).astype(jnp.bfloat16)
    return high, low


def dot(a, b, dims, precision=None):
    return lax.dot_general(
        a, b, (dims, ((), ())), precision=precision, preferred_element_type=jnp.float32
    )


def kernel(
    sizes,
    face_order_hbm,
    corner_map_hbm,
    load_table_hbm,
    basis_hbm,
    inverse_hbm,
    schur_hbm,
    neumann_hbm,
    out,
    face_order,
    corner_map,
    load_table,
    basis_in,
    inverse_in,
    schur,
    neumann,
    load,
    sol,
    face_out,
    face_in,
    basis_out,
    basis_near,
    corner_all,
    corner_flat,
    inverse_all,
    inverse_flat,
    gmat,
    spread,
    hot,
    rest_all,
    rest_flat,
    far_sem,
    local_sem,
    face_send,
    face_recv,
    basis_send,
    basis_recv,
    corner_send,
    corner_recv,
    inverse_send,
    inverse_recv,
    rest_send,
    rest_recv,
):
    subs, wides = sizes
    devices = subs * wides
    rhs, width = sol.shape[1], sol.shape[2]
    prims = basis_out.shape[1]
    order = inverse_flat.shape[0]
    owned = inverse_in.shape[0]
    row = lax.axis_index("sub")
    col = lax.axis_index("wide")
    me = row * wides + col
    has = (row > 0, row < subs - 1, col > 0, col < wides - 1)
    near = ((row - 1, col), (row + 1, col), (row, col - 1), (row, col + 1))
    share = [jnp.where(flag, jnp.float32(0.5), jnp.float32(1.0)) for flag in has]

    def place(step):
        peer = lax.rem(me + step, devices)
        return peer, (peer // wides, lax.rem(peer, wides))

    def each_peer(action):
        def one(step, carry):
            action(*place(step))
            return carry

        lax.fori_loop(1, devices, one, 0)

    load_n = pltpu.make_async_copy(neumann_hbm, neumann, local_sem.at[0])
    load_s = pltpu.make_async_copy(schur_hbm, schur, local_sem.at[1])

    pairs = (
        (face_order_hbm, face_order),
        (corner_map_hbm, corner_map),
        (load_table_hbm, load_table),
        (basis_hbm, basis_in),
        (inverse_hbm, inverse_in),
    )
    small = [
        pltpu.make_async_copy(source, target, local_sem.at[2 + i])
        for i, (source, target) in enumerate(pairs)
    ]
    for start in small:
        start.start()

    def loop(count, action):
        def one(step, carry):
            action(step)
            return carry

        lax.fori_loop(1, count, one, 0)

    def each_wide(action):
        loop(wides, lambda step: action(lax.rem(col + step, wides)))

    def each_sub(action):
        loop(subs, lambda step: action(lax.rem(row + step, subs)))

    barrier = pltpu.get_barrier_semaphore()

    def signal(sem, where):
        pl.semaphore_signal(sem, inc=1, device_id=where, device_id_type=MESH)

    each_sub(lambda other: signal(barrier, (other, col)))
    each_wide(lambda other: signal(barrier, (row, other)))

    for start in small:
        start.wait()
    basis = basis_in[...].astype(jnp.float32)
    for f in range(4):
        basis_out[f] = jnp.concatenate(
            [basis[4 * p + f : 4 * p + f + 1] for p in range(prims)], axis=0
        )
    row_of = lax.broadcasted_iota(jnp.int32, (prims, 16), 0)
    marks = jnp.zeros((prims, 16), jnp.int32)
    for p in range(prims):
        marks = jnp.where(row_of == p, corner_map[p], marks)
    corner_all[me] = marks
    table = load_table[...]
    target = 4 * lax.broadcasted_iota(jnp.int32, (rhs, table.shape[0]), 0)
    source = lax.broadcasted_iota(jnp.int32, (rhs, table.shape[0]), 1)
    for f in range(4):
        chosen = (source == target + f).astype(jnp.bfloat16)
        load[f] = dot(chosen, table, ((1,), (0,)))
        face_out[0, f] = load[f]
    inverse_all[col] = inverse_in[...]
    for f in range(4):

        @pl.when(jnp.logical_not(has[f]))
        def _():
            for turn in range(2 * ITERS):
                face_in[turn, f] = jnp.zeros((rhs, width), jnp.float32)
            basis_near[f] = jnp.zeros((prims, width), jnp.float32)

    load_n.start()
    load_s.start()
    pl.semaphore_wait(barrier, subs - 1 + wides - 1)
    each_sub(lambda other: signal(far_sem, (other, col)))

    def face_copy(turn, f):
        return pltpu.make_async_remote_copy(
            src_ref=face_out.at[turn, f],
            dst_ref=face_in.at[turn, OPPOSITE[f]],
            send_sem=face_send.at[turn, f],
            recv_sem=face_recv.at[turn, OPPOSITE[f]],
            device_id=near[f],
            device_id_type=MESH,
        )

    def face_wait(turn, f):
        pltpu.make_async_copy(
            face_out.at[turn, f], face_in.at[turn, f], face_recv.at[turn, f]
        ).wait()

    def basis_copy(f):
        return pltpu.make_async_remote_copy(
            src_ref=basis_out.at[f],
            dst_ref=basis_near.at[OPPOSITE[f]],
            send_sem=basis_send.at[f],
            recv_sem=basis_recv.at[OPPOSITE[f]],
            device_id=near[f],
            device_id_type=MESH,
        )

    def corner_copy(peer, where):
        return pltpu.make_async_remote_copy(
            src_ref=corner_all.at[me],
            dst_ref=corner_all.at[me],
            send_sem=corner_send.at[0],
            recv_sem=corner_recv.at[0],
            device_id=where,
            device_id_type=MESH,
        )

    def inverse_copy(other):
        return pltpu.make_async_remote_copy(
            src_ref=inverse_all.at[col],
            dst_ref=inverse_all.at[col],
            send_sem=inverse_send.at[other],
            recv_sem=inverse_recv.at[col],
            device_id=(row, other),
            device_id_type=MESH,
        )

    def rest_copy(iteration, peer, where):
        return pltpu.make_async_remote_copy(
            src_ref=rest_all.at[iteration, me],
            dst_ref=rest_all.at[iteration, me],
            send_sem=rest_send.at[iteration],
            recv_sem=rest_recv.at[iteration],
            device_id=where,
            device_id_type=MESH,
        )

    def wait_others(blocks, sem):
        others = blocks.at[pl.ds(0, devices - 1)]
        pltpu.make_async_copy(others, others, sem).wait()

    def send_faces(turn):
        for f in (0, 1, 2, 3):

            @pl.when(has[f])
            def _():
                face_copy(turn, f).start()

    def wait_faces(turn):
        for f in (0, 1, 2, 3):

            @pl.when(has[f])
            def _():
                face_wait(turn, f)

    for f in range(4):

        @pl.when(has[f])
        def _():
            basis_copy(f).start()

    send_faces(0)
    each_wide(lambda other: inverse_copy(other).start())
    pl.semaphore_wait(far_sem, subs - 1)
    each_peer(lambda peer, where: corner_copy(peer, where).start())

    order_of = [jnp.full((rhs, width), face_order[b], jnp.int32) for b in range(4)]
    held = [[order_of[b] == f for f in range(4)] for b in range(4)]

    def pick(masks, values):
        chosen = values[3]
        for i in range(3):
            chosen = jnp.where(masks[i], values[i], chosen)
        return chosen

    def apply_local(vectors, operator):
        blocked = jnp.concatenate(
            [pick(held[b], vectors).astype(jnp.bfloat16) for b in range(4)], axis=1
        )
        result = dot(blocked, operator[...], ((1,), (0,)))
        parts = [result[:, b * width : (b + 1) * width] for b in range(4)]
        return [pick([held[b][f] for b in range(4)], parts) for f in range(4)]

    own_basis = jnp.concatenate([basis_out[f] for f in range(4)], axis=1)
    gmat[...] = jnp.zeros(gmat.shape, jnp.float32)
    gmat[0:prims, :] = own_basis
    for f in range(4):

        @pl.when(has[f])
        def _():
            pltpu.make_async_copy(basis_near.at[f], basis_near.at[f], basis_recv.at[f]).wait()

    for f in range(4):
        gmat[(f + 1) * prims : (f + 2) * prims, f * width : (f + 1) * width] = basis_near[f]
    sides = jnp.ones((1, width), jnp.float32)
    weights = jnp.concatenate([share[f] * sides for f in range(4)], axis=1)
    shared = (gmat[...] * weights).astype(jnp.bfloat16)
    group = min(devices, 32)
    span = group * prims
    shifts = (0, -wides, wides, -1, 1)

    def restrict(values):
        high, low = split(values)
        parts = dot(shared, high, ((1,), (1,))) + dot(shared, low, ((1,), (1,)))
        return jnp.concatenate([parts[g * prims : (g + 1) * prims] for g in range(5)], axis=1)

    def mark(part):
        for g in range(5):
            for d in range(group):
                peer = jnp.clip(part * group + d + shifts[g], 0, devices - 1)
                start = g * span + d * prims
                corner_flat[start : start + prims, :] = corner_all[peer]
        lanes = lax.broadcasted_iota(jnp.int32, hot.shape, 1)
        hot[...] = (corner_flat[:, :1] == lanes).astype(jnp.float32).astype(jnp.bfloat16)

    def prepare():
        each_wide(
            lambda other: pltpu.make_async_copy(
                inverse_all.at[other], inverse_all.at[other], inverse_recv.at[other]
            ).wait()
        )
        for w in range(wides):
            inverse_flat[w * owned : (w + 1) * owned, :] = inverse_all[w]
        wait_others(corner_all, corner_recv.at[0])
        lanes = lax.broadcasted_iota(jnp.int32, (prims, order), 1)
        picks = [marks[:, :1] == lanes]
        for f in range(4):
            peer = jnp.where(has[f], near[f][0] * wides + near[f][1], me)
            picks.append(corner_all[peer][:, :1] == lanes)
        mine = jnp.concatenate([chosen.astype(jnp.float32) for chosen in picks], axis=0)
        columns = dot(mine, inverse_flat[...], ((1,), (0,)), HIGHEST)
        spread[...] = dot(columns.T, gmat[...], ((1,), (0,)), HIGHEST)
        if devices == group:
            mark(0)

    def correct(iteration):
        def one(part):
            if devices > group:
                mark(part)
            for d in range(group):
                rest_flat[d * prims : (d + 1) * prims, :] = rest_all[iteration, part * group + d]
            turned = rest_flat[...].T
            lined = jnp.concatenate([turned[g * rhs : (g + 1) * rhs] for g in range(5)], axis=1)
            high, low = split(lined)
            return dot(high, hot[...], ((1,), (0,))) + dot(low, hot[...], ((1,), (0,)))

        if devices == group:
            total = one(0)
        else:
            total = lax.fori_loop(
                0,
                devices // group,
                lambda part, total: total + one(part),
                jnp.zeros((rhs, order), jnp.float32),
            )
        return dot(total, spread[...], ((1,), (0,)), HIGHEST)

    for iteration in range(ITERS):
        first = 2 * iteration
        if iteration > 0:
            if iteration == 1:
                load_s.wait()
            local = apply_local([sol[f] for f in range(4)], schur)
            for f in range(4):
                face_out[first, f] = load[f] - local[f]
            send_faces(first)
        rest_all[iteration, me] = restrict(
            jnp.concatenate([face_out[first, f] for f in range(4)], axis=1)
        )
        each_peer(lambda peer, where: rest_copy(iteration, peer, where).start())
        wait_faces(first)
        weighted = [share[f] * (face_out[first, f] + face_in[first, f]) for f in range(4)]
        if iteration == 0:
            load_n.wait()
        local = apply_local(weighted, neumann)
        for f in range(4):
            face_out[first + 1, f] = local[f]
        send_faces(first + 1)
        if iteration == 0:
            prepare()
        wait_others(rest_all.at[iteration], rest_recv.at[iteration])
        correction = correct(iteration)
        wait_faces(first + 1)
        for f in range(4):
            update = share[f] * (
                face_out[first + 1, f]
                + face_in[first + 1, f]
                + correction[:, f * width : (f + 1) * width]
            )
            if iteration == 0:
                sol[f] = damping * update
            elif iteration < ITERS - 1:
                sol[f] = sol[f] + damping * update
            else:
                out[f] = sol[f] + damping * update

    for turn in range(2 * ITERS):
        for f in range(4):

            @pl.when(has[f])
            def _():
                face_copy(turn, f).wait_send()

    for f in range(4):

        @pl.when(has[f])
        def _():
            basis_copy(f).wait_send()

    each_wide(lambda other: inverse_copy(other).wait_send())

    wait_others(corner_all, corner_send.at[0])
    for iteration in range(ITERS):
        wait_others(rest_all.at[iteration], rest_send.at[iteration])


def expand(load_column, values, out):
    faces, patterns, width = values.shape
    rhs = out.shape[1]
    wanted = lax.broadcasted_iota(jnp.int32, (patterns, rhs), 0) == load_column[...]
    chosen = wanted.astype(jnp.float32).T.astype(jnp.bfloat16)
    whole = jnp.concatenate([values[f] for f in range(faces)], axis=1)
    high, low = split(whole)
    last = (whole - high.astype(jnp.float32) - low.astype(jnp.float32)).astype(jnp.bfloat16)
    result = (
        dot(chosen, high, ((1,), (0,)))
        + dot(chosen, low, ((1,), (0,)))
        + dot(chosen, last, ((1,), (0,)))
    )
    for f in range(faces):
        out[f] = result[:, f * width : (f + 1) * width]


def body(
    load_table, load_column, face_order, schur, neumann, coarse_basis, corner_map, coarse_inverse
):
    subs, wides = lax.axis_size("sub"), lax.axis_size("wide")
    devices = subs * wides
    patterns, width = load_table.shape[2], load_table.shape[4]
    rhs = load_column.shape[0]
    inner = schur.shape[2]
    prims = coarse_basis.shape[2]
    owned, order = coarse_inverse.shape
    assert schur.shape[0] == 1 and schur.shape[1] == 1
    f32 = jnp.float32
    group = min(devices, 32)
    dma = pltpu.SemaphoreType.DMA
    vmem = pl.BlockSpec(memory_space=pltpu.VMEM)
    hbm = pl.BlockSpec(memory_space=pl.ANY)
    result = pl.pallas_call(
        functools.partial(kernel, (subs, wides)),
        out_shape=jax.ShapeDtypeStruct((4, patterns, width), f32),
        in_specs=[hbm] * 7,
        out_specs=vmem,
        scratch_shapes=[
            pltpu.SMEM((4,), face_order.dtype),
            pltpu.SMEM((prims,), corner_map.dtype),
            pltpu.VMEM((patterns * 4, width), load_table.dtype),
            pltpu.VMEM((prims * 4, width), coarse_basis.dtype),
            pltpu.VMEM((owned, order), f32),
            pltpu.VMEM((inner, inner), schur.dtype),
            pltpu.VMEM((inner, inner), neumann.dtype),
            pltpu.VMEM((4, patterns, width), f32),
            pltpu.VMEM((4, patterns, width), f32),
            pltpu.VMEM((2 * ITERS, 4, patterns, width), f32),
            pltpu.VMEM((2 * ITERS, 4, patterns, width), f32),
            pltpu.VMEM((4, prims, width), f32),
            pltpu.VMEM((4, prims, width), f32),
            pltpu.VMEM((devices, prims, 16), jnp.int32),
            pltpu.VMEM((5 * group * prims, 16), jnp.int32),
            pltpu.VMEM((wides, owned, order), f32),
            pltpu.VMEM((order, order), f32),
            pltpu.VMEM((5 * prims, 4 * width), f32),
            pltpu.VMEM((order, 4 * width), f32),
            pltpu.VMEM((5 * group * prims, order), jnp.bfloat16),
            pltpu.VMEM((ITERS, devices, prims, 5 * patterns), f32),
            pltpu.VMEM((group * prims, 5 * patterns), f32),
            pltpu.SemaphoreType.REGULAR,
            dma((7,)),
            dma((2 * ITERS, 4)),
            dma((2 * ITERS, 4)),
            dma((4,)),
            dma((4,)),
            dma((1,)),
            dma((1,)),
            dma((wides,)),
            dma((wides,)),
            dma((ITERS,)),
            dma((ITERS,)),
        ],
        compiler_params=pltpu.CompilerParams(collective_id=0, has_side_effects=True),
        name="bddc",
    )(
        face_order.reshape(4),
        corner_map.reshape(prims),
        load_table.reshape(patterns * 4, width),
        coarse_basis.reshape(prims * 4, width),
        coarse_inverse,
        schur.reshape(inner, inner),
        neumann.reshape(inner, inner),
    )
    full = pl.pallas_call(
        expand,
        out_shape=jax.ShapeDtypeStruct((4, rhs, width), f32),
        in_specs=[vmem, vmem],
        out_specs=vmem,
        name="expand",
    )(load_column.reshape(1, rhs), result)
    return full.reshape(1, 1, 4, rhs, width)


def solution(mesh):
    in_specs = (
        P("sub", "wide", None, None, None),
        P(),
        P("sub", "wide", None),
        P("sub", "wide", None, None),
        P("sub", "wide", None, None),
        P("sub", "wide", None, None, None),
        P("sub", "wide", None),
        P("wide", None),
    )
    out_specs = P("sub", "wide", None, None, None)
    return jax.shard_map(body, mesh=mesh, in_specs=in_specs, out_specs=out_specs, check_vma=False)
```

```python
import functools

import jax
import jax.numpy as jnp
from jax import lax
from jax.experimental import pallas as pl
from jax.experimental.pallas import tpu as pltpu
from jax.sharding import PartitionSpec as P

ITERS = 3
damping = 0.3
MESH = pl.DeviceIdType.MESH
HIGHEST = lax.Precision.HIGHEST
OPPOSITE = (1, 0, 3, 2)


def split(value):
    high = value.astype(jnp.bfloat16)
    low = (value - high.astype(jnp.float32)).astype(jnp.bfloat16)
    return high, low


def dot(a, b, dims, precision=None):
    return lax.dot_general(
        a, b, (dims, ((), ())), precision=precision, preferred_element_type=jnp.float32
    )


def kernel(
    sizes,
    face_order_hbm,
    corner_map_hbm,
    load_table_hbm,
    basis_hbm,
    inverse_hbm,
    schur_hbm,
    neumann_hbm,
    out,
    face_order,
    corner_map,
    load_table,
    basis_in,
    inverse_in,
    schur,
    neumann,
    load,
    sol,
    face_out,
    face_in,
    basis_out,
    basis_near,
    corner_all,
    corner_flat,
    inverse_all,
    inverse_flat,
    gmat,
    spread,
    hot,
    rest_all,
    rest_flat,
    far_sem,
    local_sem,
    face_send,
    face_recv,
    basis_send,
    basis_recv,
    corner_send,
    corner_recv,
    inverse_send,
    inverse_recv,
    rest_send,
    rest_recv,
):
    subs, wides = sizes
    devices = subs * wides
    rhs, width = sol.shape[1], sol.shape[2]
    prims = basis_out.shape[1]
    order = inverse_flat.shape[0]
    owned = inverse_in.shape[0]
    row = lax.axis_index("sub")
    col = lax.axis_index("wide")
    me = row * wides + col
    has = (row > 0, row < subs - 1, col > 0, col < wides - 1)
    near = ((row - 1, col), (row + 1, col), (row, col - 1), (row, col + 1))
    share = [jnp.where(flag, jnp.float32(0.5), jnp.float32(1.0)) for flag in has]

    def place(step):
        peer = lax.rem(me + step, devices)
        return peer, (peer // wides, lax.rem(peer, wides))

    def each_peer(action):
        def one(step, carry):
            action(*place(step))
            return carry

        lax.fori_loop(1, devices, one, 0)

    load_n = pltpu.make_async_copy(neumann_hbm, neumann, local_sem.at[0])
    load_s = pltpu.make_async_copy(schur_hbm, schur, local_sem.at[1])

    pairs = (
        (face_order_hbm, face_order),
        (corner_map_hbm, corner_map),
        (load_table_hbm, load_table),
        (basis_hbm, basis_in),
        (inverse_hbm, inverse_in),
    )
    small = [
        pltpu.make_async_copy(source, target, local_sem.at[2 + i])
        for i, (source, target) in enumerate(pairs)
    ]
    for start in small:
        start.start()

    def loop(count, action):
        def one(step, carry):
            action(step)
            return carry

        lax.fori_loop(1, count, one, 0)

    def each_wide(action):
        loop(wides, lambda step: action(lax.rem(col + step, wides)))

    def each_sub(action):
        loop(subs, lambda step: action(lax.rem(row + step, subs)))

    barrier = pltpu.get_barrier_semaphore()

    def signal(sem, where):
        pl.semaphore_signal(sem, inc=1, device_id=where, device_id_type=MESH)

    each_sub(lambda other: signal(barrier, (other, col)))
    each_wide(lambda other: signal(barrier, (row, other)))

    for start in small:
        start.wait()
    basis = basis_in[...].astype(jnp.float32)
    for f in range(4):
        basis_out[f] = jnp.concatenate(
            [basis[4 * p + f : 4 * p + f + 1] for p in range(prims)], axis=0
        )
    row_of = lax.broadcasted_iota(jnp.int32, (prims, 16), 0)
    marks = jnp.zeros((prims, 16), jnp.int32)
    for p in range(prims):
        marks = jnp.where(row_of == p, corner_map[p], marks)
    corner_all[me] = marks
    table = load_table[...]
    target = 4 * lax.broadcasted_iota(jnp.int32, (rhs, table.shape[0]), 0)
    source = lax.broadcasted_iota(jnp.int32, (rhs, table.shape[0]), 1)
    for f in range(4):
        chosen = (source == target + f).astype(jnp.bfloat16)
        load[f] = dot(chosen, table, ((1,), (0,)))
        face_out[0, f] = load[f]
    inverse_all[col] = inverse_in[...]
    for f in range(4):

        @pl.when(jnp.logical_not(has[f]))
        def _():
            for turn in range(2 * ITERS):
                face_in[turn, f] = jnp.zeros((rhs, width), jnp.float32)
            basis_near[f] = jnp.zeros((prims, width), jnp.float32)

    load_n.start()
    load_s.start()
    pl.semaphore_wait(barrier, subs - 1 + wides - 1)
    each_sub(lambda other: signal(far_sem, (other, col)))

    def face_copy(turn, f):
        return pltpu.make_async_remote_copy(
            src_ref=face_out.at[turn, f],
            dst_ref=face_in.at[turn, OPPOSITE[f]],
            send_sem=face_send.at[turn, f],
            recv_sem=face_recv.at[turn, OPPOSITE[f]],
            device_id=near[f],
            device_id_type=MESH,
        )

    def face_wait(turn, f):
        pltpu.make_async_copy(
            face_out.at[turn, f], face_in.at[turn, f], face_recv.at[turn, f]
        ).wait()

    def basis_copy(f):
        return pltpu.make_async_remote_copy(
            src_ref=basis_out.at[f],
            dst_ref=basis_near.at[OPPOSITE[f]],
            send_sem=basis_send.at[f],
            recv_sem=basis_recv.at[OPPOSITE[f]],
            device_id=near[f],
            device_id_type=MESH,
        )

    def corner_copy(peer, where):
        return pltpu.make_async_remote_copy(
            src_ref=corner_all.at[me],
            dst_ref=corner_all.at[me],
            send_sem=corner_send.at[0],
            recv_sem=corner_recv.at[0],
            device_id=where,
            device_id_type=MESH,
        )

    def inverse_copy(other):
        return pltpu.make_async_remote_copy(
            src_ref=inverse_all.at[col],
            dst_ref=inverse_all.at[col],
            send_sem=inverse_send.at[other],
            recv_sem=inverse_recv.at[col],
            device_id=(row, other),
            device_id_type=MESH,
        )

    def rest_copy(iteration, peer, where):
        return pltpu.make_async_remote_copy(
            src_ref=rest_all.at[iteration, me],
            dst_ref=rest_all.at[iteration, me],
            send_sem=rest_send.at[iteration],
            recv_sem=rest_recv.at[iteration],
            device_id=where,
            device_id_type=MESH,
        )

    def wait_others(blocks, sem):
        others = blocks.at[pl.ds(0, devices - 1)]
        pltpu.make_async_copy(others, others, sem).wait()

    def send_faces(turn):
        for f in (0, 1, 2, 3):

            @pl.when(has[f])
            def _():
                face_copy(turn, f).start()

    def wait_faces(turn):
        for f in (0, 1, 2, 3):

            @pl.when(has[f])
            def _():
                face_wait(turn, f)

    for f in range(4):

        @pl.when(has[f])
        def _():
            basis_copy(f).start()

    send_faces(0)
    each_wide(lambda other: inverse_copy(other).start())
    pl.semaphore_wait(far_sem, subs - 1)
    each_peer(lambda peer, where: corner_copy(peer, where).start())

    order_of = [jnp.full((rhs, width), face_order[b], jnp.int32) for b in range(4)]
    held = [[order_of[b] == f for f in range(4)] for b in range(4)]

    def pick(masks, values):
        chosen = values[3]
        for i in range(3):
            chosen = jnp.where(masks[i], values[i], chosen)
        return chosen

    def apply_local(vectors, operator):
        blocked = jnp.concatenate(
            [pick(held[b], vectors).astype(jnp.bfloat16) for b in range(4)], axis=1
        )
        result = dot(blocked, operator[...], ((1,), (0,)))
        parts = [result[:, b * width : (b + 1) * width] for b in range(4)]
        return [pick([held[b][f] for b in range(4)], parts) for f in range(4)]

    own_basis = jnp.concatenate([basis_out[f] for f in range(4)], axis=1)
    gmat[...] = jnp.zeros(gmat.shape, jnp.float32)
    gmat[0:prims, :] = own_basis
    for f in range(4):

        @pl.when(has[f])
        def _():
            pltpu.make_async_copy(basis_near.at[f], basis_near.at[f], basis_recv.at[f]).wait()

    for f in range(4):
        gmat[(f + 1) * prims : (f + 2) * prims, f * width : (f + 1) * width] = basis_near[f]
    sides = jnp.ones((1, width), jnp.float32)
    weights = jnp.concatenate([share[f] * sides for f in range(4)], axis=1)
    shared = (gmat[...] * weights).astype(jnp.bfloat16)
    group = min(devices, 32)
    span = group * prims
    shifts = (0, -wides, wides, -1, 1)

    def restrict(values):
        high, low = split(values)
        both = dot(shared, jnp.concatenate([high, low], axis=0), ((1,), (1,)))
        parts = both[:, :rhs] + both[:, rhs:]
        return jnp.concatenate([parts[g * prims : (g + 1) * prims] for g in range(5)], axis=1)

    def mark(part):
        for g in range(5):
            for d in range(group):
                peer = jnp.clip(part * group + d + shifts[g], 0, devices - 1)
                start = g * span + d * prims
                corner_flat[start : start + prims, :] = corner_all[peer]
        lanes = lax.broadcasted_iota(jnp.int32, hot.shape, 1)
        hot[...] = (corner_flat[:, :1] == lanes).astype(jnp.float32).astype(jnp.bfloat16)

    def prepare():
        each_wide(
            lambda other: pltpu.make_async_copy(
                inverse_all.at[other], inverse_all.at[other], inverse_recv.at[other]
            ).wait()
        )
        for w in range(wides):
            inverse_flat[w * owned : (w + 1) * owned, :] = inverse_all[w]
        wait_others(corner_all, corner_recv.at[0])
        lanes = lax.broadcasted_iota(jnp.int32, (prims, order), 1)
        picks = [marks[:, :1] == lanes]
        for f in range(4):
            peer = jnp.where(has[f], near[f][0] * wides + near[f][1], me)
            picks.append(corner_all[peer][:, :1] == lanes)
        mine = jnp.concatenate([chosen.astype(jnp.float32) for chosen in picks], axis=0)
        columns = dot(mine, inverse_flat[...], ((1,), (0,)), HIGHEST)
        spread[0], spread[1] = split(dot(columns.T, gmat[...], ((1,), (0,)), HIGHEST))
        if devices == group:
            mark(0)

    def correct(iteration):
        def one(part):
            if devices > group:
                mark(part)
            for d in range(group):
                rest_flat[d * prims : (d + 1) * prims, :] = rest_all[iteration, part * group + d]
            turned = rest_flat[...].T
            lined = jnp.concatenate([turned[g * rhs : (g + 1) * rhs] for g in range(5)], axis=1)
            high, low = split(lined)
            both = dot(jnp.concatenate([high, low], axis=0), hot[...], ((1,), (0,)))
            return both[:rhs] + both[rhs:]

        if devices == group:
            total = one(0)
        else:
            total = lax.fori_loop(
                0,
                devices // group,
                lambda part, total: total + one(part),
                jnp.zeros((rhs, order), jnp.float32),
            )
        high, low = split(total)
        both = dot(jnp.concatenate([high, low], axis=0), spread[0], ((1,), (0,)))
        return both[:rhs] + both[rhs:] + dot(high, spread[1], ((1,), (0,)))

    for iteration in range(ITERS):
        first = 2 * iteration
        if iteration > 0:
            if iteration == 1:
                load_s.wait()
            local = apply_local([sol[f] for f in range(4)], schur)
            for f in range(4):
                face_out[first, f] = load[f] - local[f]
            send_faces(first)
        rest_all[iteration, me] = restrict(
            jnp.concatenate([face_out[first, f] for f in range(4)], axis=1)
        )
        each_peer(lambda peer, where: rest_copy(iteration, peer, where).start())
        wait_faces(first)
        weighted = [share[f] * (face_out[first, f] + face_in[first, f]) for f in range(4)]
        if iteration == 0:
            load_n.wait()
        local = apply_local(weighted, neumann)
        for f in range(4):
            face_out[first + 1, f] = local[f]
        send_faces(first + 1)
        if iteration == 0:
            prepare()
        wait_others(rest_all.at[iteration], rest_recv.at[iteration])
        correction = correct(iteration)
        wait_faces(first + 1)
        for f in range(4):
            update = share[f] * (
                face_out[first + 1, f]
                + face_in[first + 1, f]
                + correction[:, f * width : (f + 1) * width]
            )
            if iteration == 0:
                sol[f] = damping * update
            elif iteration < ITERS - 1:
                sol[f] = sol[f] + damping * update
            else:
                out[f] = sol[f] + damping * update

    for turn in range(2 * ITERS):
        for f in range(4):

            @pl.when(has[f])
            def _():
                face_copy(turn, f).wait_send()

    for f in range(4):

        @pl.when(has[f])
        def _():
            basis_copy(f).wait_send()

    each_wide(lambda other: inverse_copy(other).wait_send())

    wait_others(corner_all, corner_send.at[0])
    for iteration in range(ITERS):
        wait_others(rest_all.at[iteration], rest_send.at[iteration])


def expand(load_column, values, out):
    faces, patterns, width = values.shape
    rhs = out.shape[1]
    wanted = lax.broadcasted_iota(jnp.int32, (patterns, rhs), 0) == load_column[...]
    chosen = wanted.astype(jnp.float32).T.astype(jnp.bfloat16)
    whole = jnp.concatenate([values[f] for f in range(faces)], axis=1)
    high, low = split(whole)
    last = (whole - high.astype(jnp.float32) - low.astype(jnp.float32)).astype(jnp.bfloat16)
    result = (
        dot(chosen, high, ((1,), (0,)))
        + dot(chosen, low, ((1,), (0,)))
        + dot(chosen, last, ((1,), (0,)))
    )
    for f in range(faces):
        out[f] = result[:, f * width : (f + 1) * width]


def body(
    load_table, load_column, face_order, schur, neumann, coarse_basis, corner_map, coarse_inverse
):
    subs, wides = lax.axis_size("sub"), lax.axis_size("wide")
    devices = subs * wides
    patterns, width = load_table.shape[2], load_table.shape[4]
    rhs = load_column.shape[0]
    inner = schur.shape[2]
    prims = coarse_basis.shape[2]
    owned, order = coarse_inverse.shape
    assert schur.shape[0] == 1 and schur.shape[1] == 1
    f32 = jnp.float32
    group = min(devices, 32)
    dma = pltpu.SemaphoreType.DMA
    vmem = pl.BlockSpec(memory_space=pltpu.VMEM)
    hbm = pl.BlockSpec(memory_space=pl.ANY)
    result = pl.pallas_call(
        functools.partial(kernel, (subs, wides)),
        out_shape=jax.ShapeDtypeStruct((4, patterns, width), f32),
        in_specs=[hbm] * 7,
        out_specs=vmem,
        scratch_shapes=[
            pltpu.SMEM((4,), face_order.dtype),
            pltpu.SMEM((prims,), corner_map.dtype),
            pltpu.VMEM((patterns * 4, width), load_table.dtype),
            pltpu.VMEM((prims * 4, width), coarse_basis.dtype),
            pltpu.VMEM((owned, order), f32),
            pltpu.VMEM((inner, inner), schur.dtype),
            pltpu.VMEM((inner, inner), neumann.dtype),
            pltpu.VMEM((4, patterns, width), f32),
            pltpu.VMEM((4, patterns, width), f32),
            pltpu.VMEM((2 * ITERS, 4, patterns, width), f32),
            pltpu.VMEM((2 * ITERS, 4, patterns, width), f32),
            pltpu.VMEM((4, prims, width), f32),
            pltpu.VMEM((4, prims, width), f32),
            pltpu.VMEM((devices, prims, 16), jnp.int32),
            pltpu.VMEM((5 * group * prims, 16), jnp.int32),
            pltpu.VMEM((wides, owned, order), f32),
            pltpu.VMEM((order, order), f32),
            pltpu.VMEM((5 * prims, 4 * width), f32),
            pltpu.VMEM((2, order, 4 * width), jnp.bfloat16),
            pltpu.VMEM((5 * group * prims, order), jnp.bfloat16),
            pltpu.VMEM((ITERS, devices, prims, 5 * patterns), f32),
            pltpu.VMEM((group * prims, 5 * patterns), f32),
            pltpu.SemaphoreType.REGULAR,
            dma((7,)),
            dma((2 * ITERS, 4)),
            dma((2 * ITERS, 4)),
            dma((4,)),
            dma((4,)),
            dma((1,)),
            dma((1,)),
            dma((wides,)),
            dma((wides,)),
            dma((ITERS,)),
            dma((ITERS,)),
        ],
        compiler_params=pltpu.CompilerParams(collective_id=0, has_side_effects=True),
        name="bddc",
    )(
        face_order.reshape(4),
        corner_map.reshape(prims),
        load_table.reshape(patterns * 4, width),
        coarse_basis.reshape(prims * 4, width),
        coarse_inverse,
        schur.reshape(inner, inner),
        neumann.reshape(inner, inner),
    )
    full = pl.pallas_call(
        expand,
        out_shape=jax.ShapeDtypeStruct((4, rhs, width), f32),
        in_specs=[vmem, vmem],
        out_specs=vmem,
        name="expand",
    )(load_column.reshape(1, rhs), result)
    return full.reshape(1, 1, 4, rhs, width)


def solution(mesh):
    in_specs = (
        P("sub", "wide", None, None, None),
        P(),
        P("sub", "wide", None),
        P("sub", "wide", None, None),
        P("sub", "wide", None, None),
        P("sub", "wide", None, None, None),
        P("sub", "wide", None),
        P("wide", None),
    )
    out_specs = P("sub", "wide", None, None, None)
    return jax.shard_map(body, mesh=mesh, in_specs=in_specs, out_specs=out_specs, check_vma=False)
```
